1024 devices in a mesh: gx: 32 (over y_lo, z, core), fam: 32 (over x, y_hi).
Axes of the slice: x: 8, y: 8 (y_hi: 4, y_lo: 2; y = y_hi * 2 + y_lo), z: 8, core: 2. Of those that a mesh axis runs over, the one named last changes fastest.
Arguments:
- labels: int32 [1, 512, 512], P(None, 'gx'), may hold values from 0 to 2047, as said below
- family_of_grain: int32 [2048], replicated, may hold values from 0 to 255
Outputs:
- distance: float32 [256, 1, 512, 512], P('fam', None, 'gx')
The draws below stay inside these ranges and needn't reach their ends.
Inputs may be any that keep to these rules, and one draw needn't show every extreme that they name: `labels`: cells lie mostly in square grains of 32 x 32 cells; about a quarter of the cells carry some other grain.
All inputs are finite; a program needn't handle non-finite values.
Results may differ from the reference program's by a relative error of at most 0.0019.
Values may be sent and summed in bfloat16 or wider, within the bound.
No kernel may reach another device: no remote copies, remote signals or barrier semaphores. Data moves between devices by JAX's collectives and lax.ppermute only.
A program may use at most 32 MiB of HBM per device.

```python
import jax
import jax.numpy as jnp
from jax import lax

F = 256
NX = 512
NY = 512
NZ = 1
GRAINS = 2048
BLOCK = 32
WIDTH = 2
SWEEPS = 3


def draw_labels(key, part):
    first = jax.random.fold_in(key, 11)
    second = jax.random.fold_in(key, 12)
    third = jax.random.fold_in(key, 13)
    coarse = jax.random.randint(first, (NZ, NX // BLOCK, NY // BLOCK), 0, GRAINS)
    coarse = jnp.repeat(jnp.repeat(coarse, BLOCK, axis=1), BLOCK, axis=2)
    flip = jax.random.randint(second, (NZ, NX, NY), 0, 4) == 0
    other = jax.random.randint(third, (NZ, NX, NY), 0, GRAINS)
    return jnp.where(flip, other, coarse).astype(jnp.int32)


def set_ends(result, rng, least, high):
    spot = [jax.random.randint(jax.random.fold_in(rng, axis), (), 0, length) for axis, length in enumerate(result.shape)]
    main_axis = result.shape.index(max(result.shape))
    beside = spot[:main_axis] + [(spot[main_axis] + 1) % result.shape[main_axis]] + spot[main_axis + 1:]
    return result.at[tuple(spot)].set(least).at[tuple(beside)].set(high)


def setup_inputs(seed: int = 0) -> dict:
    key_of = jax.random.split(jax.random.key(seed), 3)
    return {
        "labels": draw_labels(jax.random.fold_in(key_of[2], 71), 0),
        "family_of_grain": set_ends(jax.random.randint(key_of[1], (GRAINS,), 0, F), jax.random.fold_in(key_of[1], 1), 0, F - 1).astype(jnp.int32),
    }


fidelity = 0.25
scale_factor = 8.0
step_size = 0.5

def cas_table(count):
    idx = jnp.arange(count).astype(jnp.float32)
    angle = 2.0 * jnp.pi * jnp.outer(idx, idx) / count
    return (jnp.cos(angle) + jnp.sin(angle)).astype(jnp.bfloat16)

def gauss_table(count):
    freq = jnp.arange(count)
    mirror = jnp.minimum(freq, count - freq).astype(jnp.float32)
    sigma = WIDTH / 2.0
    return jnp.exp(-2.0 * jnp.pi ** 2 * sigma ** 2 * mirror ** 2 / (count * count))

def godunov(ext, sign):
    centre = ext[:, :, 1:-1]
    pairs = [(centre - ext[:, :, :-2], ext[:, :, 2:] - centre), (centre - jnp.roll(centre, 1, 3), jnp.roll(centre, -1, 3) - centre), (centre - jnp.roll(centre, 1, 1), jnp.roll(centre, -1, 1) - centre)]
    plus = jnp.zeros_like(centre)
    minus = jnp.zeros_like(centre)
    for back, fore in pairs:
        plus = plus + jnp.maximum(jnp.maximum(back, 0.0) ** 2, jnp.minimum(fore, 0.0) ** 2)
        minus = minus + jnp.maximum(jnp.minimum(back, 0.0) ** 2, jnp.maximum(fore, 0.0) ** 2)
    grad = jnp.sqrt(jnp.where(sign > 0, plus, minus))
    return centre - step_size * sign * (grad - 1.0)

def reference(labels, family_of_grain):
    group = 8
    owner = jnp.take(family_of_grain, labels, axis=0)
    cas_x = cas_table(NX).astype(jnp.float32)
    cas_y = cas_table(NY).astype(jnp.float32)
    gauss_x = gauss_table(NX)
    gauss_y = gauss_table(NY)

    def smooth_group(start):
        ids = start + jnp.arange(group)
        chi = (owner[None] == ids[:, None, None, None]).astype(jnp.bfloat16)
        spec_y = (jnp.einsum('fzxy,yk->fzxk', chi.astype(jnp.float32), cas_y) * gauss_y).astype(jnp.bfloat16)
        spec_xy = (jnp.einsum('fzxk,xq->fzqk', spec_y.astype(jnp.float32), cas_x) * gauss_x[None, None, :, None]).astype(jnp.bfloat16)
        back_x = (jnp.einsum('fzqk,qx->fzxk', spec_xy.astype(jnp.float32), cas_x) * (1.0 / NX)).astype(jnp.bfloat16)
        smooth = jnp.einsum('fzxk,ky->fzxy', back_x.astype(jnp.float32), cas_y) * (1.0 / NY)
        return smooth + fidelity * chi.astype(jnp.float32)

    def first_pass(carry, start):
        high, second = carry
        u = smooth_group(start)
        for j in range(group):
            second = jnp.maximum(jnp.minimum(high, u[j]), second)
            high = jnp.maximum(high, u[j])
        return ((high, second), u)
    lowest = jnp.full((NZ, NX, NY), -1e+30, jnp.float32)
    starts = (jnp.arange(F // group) * group).astype(jnp.int32)
    (top1, top2), u_all = lax.scan(first_pass, (lowest, lowest), starts)

    def finish(u):
        phi0 = scale_factor * (u - jnp.where(u >= top1, top2, top1))
        sign = phi0 / jnp.sqrt(phi0 * phi0 + 1.0)
        phi = phi0
        for sweep in range(SWEEPS):
            ext = jnp.pad(phi, ((0, 0), (0, 0), (1, 1), (0, 0)), mode='wrap')
            phi = godunov(ext, sign)
        return phi
    out = lax.map(finish, u_all)
    return out.reshape(F, NZ, NX, NY)
```

```python
import functools

import jax
import jax.numpy as jnp
import numpy as np
from jax import lax
from jax.experimental import pallas as pl
from jax.experimental.pallas import tpu as pltpu
from jax.sharding import Mesh, PartitionSpec as P

F = 256
NX = 512
NY = 512
GRAINS = 2048
WIDTH = 2
SWEEPS = 3

fidelity = 0.25
scale_factor = 8.0
step_size = 0.5

SLAB = 16
HALO = 4
ROWS = SLAB + 2 * HALO
OWN = 8
SHARE = 4
PEERS = 8
LOWEST = -1e30


def smoothing_operator(count):
    idx = np.arange(count, dtype=np.float32)
    angle = np.float32(2.0 * np.pi) * np.outer(idx, idx) / np.float32(count)
    angle = angle.astype(np.float64)
    cas = (np.cos(angle) + np.sin(angle)).astype(np.float32).astype(jnp.bfloat16).astype(np.float64)
    mirror = np.minimum(np.arange(count), count - np.arange(count)).astype(np.float64)
    gauss = np.exp(-2.0 * np.pi**2 * (WIDTH / 2.0) ** 2 * mirror**2 / count**2)
    full = (cas * gauss) @ cas / count
    high = full.astype(np.float32).astype(jnp.bfloat16)
    low = (full - high.astype(np.float64)).astype(np.float32).astype(jnp.bfloat16)
    return high, low


def lookup_kernel(labels_ref, table_ref, out_ref):
    rows, cols = labels_ref.shape
    for r in range(0, rows, 8):
        for c in range(0, cols, 128):
            label = labels_ref[r : r + 8, c : c + 128]
            lane = label & 127
            part = label >> 7
            owner = jnp.zeros((8, 128), jnp.int32)
            for k in range(GRAINS // 128):
                line = jnp.broadcast_to(table_ref[k : k + 1, :], (8, 128))
                owner = jnp.where(part == k, jnp.take_along_axis(line, lane, axis=1), owner)
            value = owner.astype(jnp.float32).astype(jnp.bfloat16)
            for p in range(out_ref.shape[0]):
                out_ref[p, r : r + 8, c : c + 128] = value


def halves():
    index = 0
    for r in range(0, ROWS, 4):
        for c in range(0, NY, 128):
            yield index // 3, index % 3, r, c
            index += 1


def rank_kernel(where_ref, owner_ref, high_ref, low_ref, u_ref, pair_ref, xh_ref, xl_ref, us_ref, best_ref):
    start = where_ref[0] * SLAB - HALO
    first = where_ref[1] * (SHARE * OWN)
    mine = where_ref[2]
    row = lax.broadcasted_iota(jnp.int32, (ROWS, NX), 0)
    col = lax.broadcasted_iota(jnp.int32, (ROWS, NX), 1)
    pick = jnp.where(((row + (start + NX)) & (NX - 1)) == col, 1.0, 0.0).astype(jnp.bfloat16)
    dot = functools.partial(jnp.dot, preferred_element_type=jnp.float32)
    left = jnp.concatenate([dot(pick, high_ref[...]), dot(pick, low_ref[...])], axis=0).astype(jnp.bfloat16)
    near = dot(pick, owner_ref[...])
    best_ref[0] = jnp.full((ROWS, NY), LOWEST, jnp.float32)
    best_ref[1] = jnp.full((ROWS, NY), LOWEST, jnp.float32)

    def group(q, carry):
        base = first + q * OWN
        for j in range(OWN):
            fam = (base + j).astype(jnp.float32)
            chi = jnp.where(owner_ref[...] == fam.astype(jnp.bfloat16), 1.0, 0.0).astype(jnp.bfloat16)
            both = dot(left, chi)
            mixed = both[:ROWS] + both[ROWS:]
            upper = mixed.astype(jnp.bfloat16)
            xh_ref[j * ROWS : (j + 1) * ROWS, :] = upper
            xl_ref[j * ROWS : (j + 1) * ROWS, :] = (mixed - upper.astype(jnp.float32)).astype(jnp.bfloat16)
        us_ref[...] = (
            dot(xh_ref[...], high_ref[...]) + dot(xh_ref[...], low_ref[...]) + dot(xl_ref[...], high_ref[...])
        )
        top, second = best_ref[0], best_ref[1]
        for j in range(OWN):
            fam = (base + j).astype(jnp.float32)
            u = us_ref[j * ROWS : (j + 1) * ROWS, :] + jnp.where(near == fam, fidelity, 0.0)
            us_ref[j * ROWS : (j + 1) * ROWS, :] = u
            second = jnp.maximum(jnp.minimum(top, u), second)
            top = jnp.maximum(top, u)
        best_ref[0] = top
        best_ref[1] = second

        @pl.when(q == mine)
        def _():
            u_ref[...] = us_ref[...]

        return carry

    lax.fori_loop(0, SHARE, group, 0)
    for p, s, r, c in halves():
        for k in range(2):
            pair_ref[p, 12 * k + 4 * s : 12 * k + 4 * s + 4, :] = best_ref[k, r : r + 4, c : c + 128]


def merge_kernel(pair_ref, out_ref):
    top, second = pair_ref[0, 0:12, :], pair_ref[0, 12:24, :]
    for p in range(1, PEERS):
        other, runner = pair_ref[p, 0:12, :], pair_ref[p, 12:24, :]
        second = jnp.maximum(jnp.minimum(top, other), jnp.maximum(second, runner))
        top = jnp.maximum(top, other)
    for p in range(PEERS):
        out_ref[p, 0:12, :] = top
        out_ref[p, 12:24, :] = second


def sweep_kernel(u_ref, pair_ref, out_ref, best_ref):
    for p, s, r, c in halves():
        for k in range(2):
            best_ref[k, r : r + 4, c : c + 128] = pair_ref[p, 12 * k + 4 * s : 12 * k + 4 * s + 4, :]

    def family(j, carry):
        u = u_ref[pl.ds(pl.multiple_of(j * ROWS, 8), ROWS), :]
        top, second = best_ref[0], best_ref[1]
        phi = scale_factor * (u - jnp.where(u >= top, second, top))
        sign = phi * lax.rsqrt(phi * phi + 1.0)
        side = jnp.where(sign > 0, 1.0, -1.0)
        pull = step_size * sign
        for _ in range(SWEEPS):
            slope = None
            for axis, length in ((0, ROWS), (1, NY)):
                back = phi - pltpu.roll(phi, 1, axis)
                fore = pltpu.roll(back, length - 1, axis)
                steep = jnp.maximum(jnp.maximum(side * back, -(side * fore)), 0.0)
                slope = steep * steep if slope is None else slope + steep * steep
            phi = phi - pull * (jnp.sqrt(slope) - 1.0)
        out_ref[j, 0, :, :] = phi[HALO : HALO + SLAB, :]
        return carry

    lax.fori_loop(0, OWN, family, 0)


VMEM = pl.BlockSpec(memory_space=pltpu.VMEM)
SMEM = pl.BlockSpec(memory_space=pltpu.SMEM)


def body(labels, family_of_grain):
    lines = lax.axis_size(("ylo", "z", "core"))
    gx = lax.axis_index(("ylo", "z", "core"))
    owner = pl.pallas_call(
        lookup_kernel,
        out_shape=jax.ShapeDtypeStruct((lines, SLAB, NY), jnp.bfloat16),
        in_specs=[VMEM, VMEM],
        out_specs=VMEM,
        name="lookup",
    )(labels.reshape(SLAB, NY), family_of_grain.reshape(GRAINS // 128, 128))
    owner = lax.all_to_all(owner, ("ylo", "z", "core"), split_axis=0, concat_axis=0, tiled=True)
    where = jnp.stack([gx, lax.axis_index("x"), lax.axis_index("yhi")]).astype(jnp.int32)
    high, low = smoothing_operator(NX)
    u, pairs = pl.pallas_call(
        rank_kernel,
        out_shape=(
            jax.ShapeDtypeStruct((OWN * ROWS, NY), jnp.float32),
            jax.ShapeDtypeStruct((PEERS, 24, 128), jnp.float32),
        ),
        in_specs=[SMEM, VMEM, VMEM, VMEM],
        out_specs=(VMEM, VMEM),
        scratch_shapes=[
            pltpu.VMEM((OWN * ROWS, NY), jnp.bfloat16),
            pltpu.VMEM((OWN * ROWS, NY), jnp.bfloat16),
            pltpu.VMEM((OWN * ROWS, NY), jnp.float32),
            pltpu.VMEM((2, ROWS, NY), jnp.float32),
        ],
        name="rank",
    )(where, owner.reshape(NX, NY), jnp.asarray(high), jnp.asarray(low))
    pairs = lax.all_to_all(pairs, "x", split_axis=0, concat_axis=0, tiled=True)
    pairs = pl.pallas_call(
        merge_kernel,
        out_shape=jax.ShapeDtypeStruct((PEERS, 24, 128), jnp.float32),
        in_specs=[VMEM],
        out_specs=VMEM,
        name="merge",
    )(pairs)
    pairs = lax.all_to_all(pairs, "x", split_axis=0, concat_axis=0, tiled=True)
    return pl.pallas_call(
        sweep_kernel,
        out_shape=jax.ShapeDtypeStruct((OWN, 1, SLAB, NY), jnp.float32),
        in_specs=[VMEM, VMEM],
        out_specs=VMEM,
        scratch_shapes=[pltpu.VMEM((2, ROWS, NY), jnp.float32)],
        name="sweep",
    )(u, pairs)


def solution(mesh):
    fine = Mesh(mesh.devices.reshape(2, 8, 2, PEERS, SHARE), ("ylo", "z", "core", "x", "yhi"))
    lines, fams = ("ylo", "z", "core"), ("x", "yhi")
    return jax.shard_map(
        body,
        mesh=fine,
        in_specs=(P(None, lines, None), P()),
        out_specs=P(fams, None, lines, None),
        check_vma=False,
    )
```

```python
import functools

import jax
import jax.numpy as jnp
import numpy as np
from jax import lax
from jax.experimental import pallas as pl
from jax.experimental.pallas import tpu as pltpu
from jax.sharding import Mesh, PartitionSpec as P

F = 256
NX = 512
NY = 512
GRAINS = 2048
WIDTH = 2
SWEEPS = 3

fidelity = 0.25
scale_factor = 8.0
step_size = 0.5

SLAB = 16
HALO = 4
ROWS = SLAB + 2 * HALO
OWN = 8
SHARE = 4
PEERS = 8
LOWEST = -1e30
CODE = 16384.0
LINES = ("ylo", "z", "core")


def smoothing_operator(count):
    idx = np.arange(count, dtype=np.float32)
    angle = np.float32(2.0 * np.pi) * np.outer(idx, idx) / np.float32(count)
    angle = angle.astype(np.float64)
    cas = (np.cos(angle) + np.sin(angle)).astype(np.float32).astype(jnp.bfloat16).astype(np.float64)
    mirror = np.minimum(np.arange(count), count - np.arange(count)).astype(np.float64)
    gauss = np.exp(-2.0 * np.pi**2 * (WIDTH / 2.0) ** 2 * mirror**2 / count**2)
    full = (cas * gauss) @ cas / count
    high = full.astype(np.float32).astype(jnp.bfloat16)
    low = (full - high.astype(np.float64)).astype(np.float32).astype(jnp.bfloat16)
    return high, low


def lookup_kernel(labels_ref, table_ref, out_ref):
    rows, cols = labels_ref.shape
    for r in range(0, rows, 8):
        for c in range(0, cols, 128):
            label = labels_ref[r : r + 8, c : c + 128]
            lane = label & 127
            part = label >> 7
            owner = jnp.zeros((8, 128), jnp.int32)
            for k in range(GRAINS // 128):
                line = jnp.broadcast_to(table_ref[k : k + 1, :], (8, 128))
                owner = jnp.where(part == k, jnp.take_along_axis(line, lane, axis=1), owner)
            value = owner.astype(jnp.float32).astype(jnp.bfloat16)
            for p in range(out_ref.shape[0]):
                out_ref[p, r : r + 8, c : c + 128] = value


def rank_kernel(owner_ref, high_ref, low_ref, u_ref, pair_ref, xh_ref, xl_ref, us_ref, best_ref):
    start = lax.axis_index(LINES) * SLAB - HALO
    first = lax.axis_index("x") * (SHARE * OWN)
    mine = lax.axis_index("yhi")
    row = lax.broadcasted_iota(jnp.int32, (ROWS, NX), 0)
    col = lax.broadcasted_iota(jnp.int32, (ROWS, NX), 1)
    pick = jnp.where(((row + (start + NX)) & (NX - 1)) == col, 1.0, 0.0).astype(jnp.bfloat16)
    dot = functools.partial(jnp.dot, preferred_element_type=jnp.float32)
    left = jnp.concatenate([dot(pick, high_ref[...]), dot(pick, low_ref[...])], axis=0).astype(jnp.bfloat16)
    near = dot(pick, owner_ref[...])
    one, zero = jnp.ones((), jnp.bfloat16), jnp.zeros((), jnp.bfloat16)
    best_ref[0] = jnp.full((ROWS, NY), LOWEST, jnp.float32)
    best_ref[1] = jnp.full((ROWS, NY), LOWEST, jnp.float32)

    def group(q, carry):
        base = first + q * OWN
        for j in range(OWN):
            fam = (base + j).astype(jnp.float32)
            chi = jnp.where(owner_ref[...] == fam.astype(jnp.bfloat16), one, zero)
            both = dot(left, chi)
            mixed = both[:ROWS] + both[ROWS:]
            upper = mixed.astype(jnp.bfloat16)
            xh_ref[j * ROWS : (j + 1) * ROWS, :] = upper
            xl_ref[j * ROWS : (j + 1) * ROWS, :] = (mixed - upper.astype(jnp.float32)).astype(jnp.bfloat16)
        us_ref[...] = (
            dot(xh_ref[...], high_ref[...]) + dot(xh_ref[...], low_ref[...]) + dot(xl_ref[...], high_ref[...])
        )
        top, second = best_ref[0], best_ref[1]
        for j in range(OWN):
            fam = (base + j).astype(jnp.float32)
            u = us_ref[j * ROWS : (j + 1) * ROWS, :] + jnp.where(near == fam, fidelity, 0.0)
            us_ref[j * ROWS : (j + 1) * ROWS, :] = u
            second = jnp.maximum(jnp.minimum(top, u), second)
            top = jnp.maximum(top, u)
        best_ref[0] = top
        best_ref[1] = second

        @pl.when(q == mine)
        def _():
            u_ref[...] = us_ref[...]

        return carry

    lax.fori_loop(0, SHARE, group, 0)
    for k in range(2):
        code = jnp.round(best_ref[k] * CODE).astype(jnp.int32).astype(jnp.int16)
        for p in range(PEERS):
            pair_ref[p, k] = code


def sweep_kernel(u_ref, pair_ref, out_ref, best_ref):
    top, second = pair_ref[0, 0].astype(jnp.int32), pair_ref[0, 1].astype(jnp.int32)
    for p in range(1, PEERS):
        other, runner = pair_ref[p, 0].astype(jnp.int32), pair_ref[p, 1].astype(jnp.int32)
        second = jnp.maximum(jnp.minimum(top, other), jnp.maximum(second, runner))
        top = jnp.maximum(top, other)
    best_ref[0] = top.astype(jnp.float32)
    best_ref[1] = second.astype(jnp.float32)

    def family(j, carry):
        u = u_ref[pl.ds(pl.multiple_of(j * ROWS, 8), ROWS), :]
        rival = jnp.where(jnp.round(u * CODE) >= best_ref[0], best_ref[1], best_ref[0])
        phi = scale_factor * (u - rival * (1.0 / CODE))
        sign = phi * lax.rsqrt(phi * phi + 1.0)
        side = jnp.where(sign > 0, 1.0, -1.0)
        pull = step_size * sign
        for _ in range(SWEEPS):
            slope = None
            for axis, length in ((0, ROWS), (1, NY)):
                back = phi - pltpu.roll(phi, 1, axis)
                fore = pltpu.roll(back, length - 1, axis)
                steep = jnp.maximum(jnp.maximum(side * back, -(side * fore)), 0.0)
                slope = steep * steep if slope is None else slope + steep * steep
            grad = slope * lax.rsqrt(jnp.maximum(slope, 1e-30))
            phi = phi - pull * (grad - 1.0)
        out_ref[j, 0, :, :] = phi[HALO : HALO + SLAB, :]
        return carry

    lax.fori_loop(0, OWN, family, 0, unroll=2)


VMEM = pl.BlockSpec(memory_space=pltpu.VMEM)
SMEM = pl.BlockSpec(memory_space=pltpu.SMEM)


PARAMS = pltpu.CompilerParams(vmem_limit_bytes=8 << 20)


def body(labels, family_of_grain):
    lines = lax.axis_size(LINES)
    owner = pl.pallas_call(
        lookup_kernel,
        out_shape=jax.ShapeDtypeStruct((lines, SLAB, NY), jnp.bfloat16),
        in_specs=[VMEM, VMEM],
        out_specs=VMEM,
        compiler_params=PARAMS,
        name="lookup",
    )(labels.reshape(SLAB, NY), family_of_grain.reshape(GRAINS // 128, 128))
    owner = lax.all_to_all(owner, LINES, split_axis=0, concat_axis=0, tiled=True)
    high, low = smoothing_operator(NX)
    u, pairs = pl.pallas_call(
        rank_kernel,
        out_shape=(
            jax.ShapeDtypeStruct((OWN * ROWS, NY), jnp.float32),
            jax.ShapeDtypeStruct((PEERS, 2, ROWS, NY), jnp.int16),
        ),
        in_specs=[VMEM, VMEM, VMEM],
        out_specs=(VMEM, VMEM),
        scratch_shapes=[
            pltpu.VMEM((OWN * ROWS, NY), jnp.bfloat16),
            pltpu.VMEM((OWN * ROWS, NY), jnp.bfloat16),
            pltpu.VMEM((OWN * ROWS, NY), jnp.float32),
            pltpu.VMEM((2, ROWS, NY), jnp.float32),
        ],
        compiler_params=PARAMS,
        name="rank",
    )(owner.reshape(NX, NY), jnp.asarray(high), jnp.asarray(low))
    pairs = lax.all_to_all(pairs, "x", split_axis=0, concat_axis=0, tiled=True)
    return pl.pallas_call(
        sweep_kernel,
        out_shape=jax.ShapeDtypeStruct((OWN, 1, SLAB, NY), jnp.float32),
        in_specs=[VMEM, VMEM],
        out_specs=VMEM,
        scratch_shapes=[pltpu.VMEM((2, ROWS, NY), jnp.float32)],
        compiler_params=PARAMS,
        name="sweep",
    )(u, pairs)


def solution(mesh):
    fine = Mesh(mesh.devices.reshape(2, 8, 2, PEERS, SHARE), LINES + ("x", "yhi"))
    return jax.shard_map(
        body,
        mesh=fine,
        in_specs=(P(None, LINES, None), P()),
        out_specs=P(("x", "yhi"), None, LINES, None),
        check_vma=False,
    )
```

```python
import functools

import jax
import jax.numpy as jnp
import numpy as np
from jax import lax
from jax.experimental import pallas as pl
from jax.experimental.pallas import tpu as pltpu
from jax.sharding import Mesh, PartitionSpec as P

F = 256
NX = 512
NY = 512
GRAINS = 2048
WIDTH = 2
SWEEPS = 3

fidelity = 0.25
scale_factor = 8.0
step_size = 0.5

SLAB = 16
HALO = 4
ROWS = SLAB + 2 * HALO
OWN = 8
SHARE = 4
HALF = F // 2
STEPS = HALF // OWN
CHUNKS = 4
PART = HALF // CHUNKS
TILES = NY // 128
LOWEST = -1e30
GAIN = 512.0
FINE = 32.0
LINES = ("ylo", "z", "core")
FAMS = ("x", "yhi")

dot = functools.partial(jnp.dot, preferred_element_type=jnp.float32)


def smoothing_operator(count):
    idx = np.arange(count, dtype=np.float32)
    angle = np.float32(2.0 * np.pi) * np.outer(idx, idx) / np.float32(count)
    angle = angle.astype(np.float64)
    cas = (np.cos(angle) + np.sin(angle)).astype(np.float32).astype(jnp.bfloat16).astype(np.float64)
    mirror = np.minimum(np.arange(count), count - np.arange(count)).astype(np.float64)
    gauss = np.exp(-2.0 * np.pi**2 * (WIDTH / 2.0) ** 2 * mirror**2 / count**2)
    full = (cas * gauss) @ cas / count
    high = full.astype(np.float32).astype(jnp.bfloat16)
    low = (full - high.astype(np.float64)).astype(np.float32).astype(jnp.bfloat16)
    return [part.reshape(count, TILES, 128).transpose(1, 0, 2) for part in (high, low)]


def lookup_kernel(labels_hbm, table_hbm, out_ref, labels_ref, table_ref, sems):
    copies = [
        pltpu.make_async_copy(labels_hbm, labels_ref, sems.at[0]),
        pltpu.make_async_copy(table_hbm, table_ref, sems.at[1]),
    ]
    for copy in copies:
        copy.start()
    for copy in copies:
        copy.wait()
    for c in range(TILES):
        for r in range(0, SLAB, 8):
            label = labels_ref[r : r + 8, c * 128 : (c + 1) * 128]
            lane = label & 127
            part = label >> 7
            owner = jnp.zeros((8, 128), jnp.int32)
            for k in range(GRAINS // 128):
                line = jnp.broadcast_to(table_ref[k : k + 1, :], (8, 128))
                owner = jnp.where(part == k, jnp.take_along_axis(line, lane, axis=1), owner)
            value = owner.astype(jnp.float32).astype(jnp.bfloat16)
            for p in range(out_ref.shape[0]):
                out_ref[p, c, r : r + 8, :] = value


def blocks(ref):
    return jnp.concatenate([ref[c] for c in range(TILES)], axis=1)


def owners(owner_ref, first, count):
    return jnp.concatenate([owner_ref[:, c].reshape(NX, 128) for c in range(first, first + count)], axis=1)


def selector(start, rows):
    row = lax.broadcasted_iota(jnp.int32, (rows, NX), 0)
    col = lax.broadcasted_iota(jnp.int32, (rows, NX), 1)
    return jnp.where(((row + (start + NX)) & (NX - 1)) == col, 1.0, 0.0).astype(jnp.bfloat16)


def one_hot(owner, fam):
    one, zero = jnp.ones((), jnp.bfloat16), jnp.zeros((), jnp.bfloat16)
    return jnp.where(owner == fam.astype(jnp.float32).astype(jnp.bfloat16), one, zero)


def rank_kernel(owner_ref, high_ref, low_ref, keep_ref, send_ref, left_ref, near_ref, id_ref, x_ref, best_ref, *u_refs):
    f8 = jnp.float8_e4m3fn
    x = lax.axis_index("x")
    mine = (x >> 1) * SHARE + lax.axis_index("yhi")
    pick = selector(lax.axis_index(LINES) * SLAB - HALO, ROWS)
    one, zero = jnp.ones((), f8), jnp.zeros((), f8)
    for h in range(2):
        cols = slice(h * 256, (h + 1) * 256)
        table = jnp.concatenate([high_ref[2 * h], high_ref[2 * h + 1]], axis=1)
        rest = jnp.concatenate([low_ref[2 * h], low_ref[2 * h + 1]], axis=1)
        left = (dot(pick, table) + dot(pick, rest)) * GAIN
        coarse = left.astype(f8)
        left_ref[:, cols] = jnp.concatenate(
            [coarse, ((left - coarse.astype(jnp.float32)) * FINE).astype(f8)], axis=0
        )
        owner = owners(owner_ref, 2 * h, 2)
        near_ref[:, cols] = dot(pick, owner)
        id_ref[:, cols] = (owner.astype(jnp.float32).astype(jnp.int32) - 128).astype(jnp.int8)

    def block_of(step):
        turn = jnp.where(step == STEPS - 1, mine, step + (step >= mine).astype(jnp.int32))
        return (((x & 1) + 2 * (turn // SHARE)) * SHARE + turn % SHARE) * OWN

    def mix(step, carry):
        base = block_of(step)
        left = left_ref[...]
        at = pl.multiple_of(step * (OWN * ROWS), 16)
        for h in range(2):
            cols = slice(h * 256, (h + 1) * 256)
            owner = id_ref[:, cols]
            parts = []
            for j in range(OWN):
                both = dot(left, jnp.where(owner == (base + j - 128).astype(jnp.int8), one, zero))
                parts.append(both[:ROWS] + both[ROWS:] * (1.0 / FINE))
            x_ref[pl.ds(at, OWN * ROWS), cols] = jnp.concatenate(parts, axis=0).astype(jnp.bfloat16)
        return carry

    lax.fori_loop(0, STEPS, mix, 0)
    best_ref[...] = jnp.full((2, ROWS, NY), LOWEST, jnp.float32)
    table = blocks(high_ref)
    for chunk in range(CHUNKS):
        u_ref = u_refs[chunk % 2]
        u_ref[...] = dot(x_ref[chunk * PART * ROWS : (chunk + 1) * PART * ROWS, :], table)
        for c in range(TILES):
            cols = slice(c * 128, (c + 1) * 128)
            near = near_ref[:, cols]
            top, second = best_ref[0, :, cols], best_ref[1, :, cols]
            for j in range(PART):
                index = chunk * PART + j
                if index == HALF - OWN:
                    keep_ref[0, :, cols] = top * (1.0 / GAIN)
                    keep_ref[1, :, cols] = second * (1.0 / GAIN)
                fam = (block_of(index // OWN) + index % OWN).astype(jnp.float32)
                u = u_ref[j * ROWS : (j + 1) * ROWS, cols] + jnp.where(near == fam, fidelity * GAIN, 0.0)
                second = jnp.maximum(jnp.minimum(top, u), second)
                top = jnp.maximum(top, u)
            best_ref[0, :, cols] = top
            best_ref[1, :, cols] = second
    send_ref[...] = best_ref[...] * (1.0 / GAIN)


def own_kernel(owner_ref, high_ref, low_ref, u_ref, x_ref, xl_ref):
    base = lax.axis_index(FAMS) * OWN
    pick = selector(lax.axis_index(LINES) * SLAB - HALO, ROWS)
    high, low = blocks(high_ref), blocks(low_ref)
    left = jnp.concatenate([dot(pick, high), dot(pick, low)], axis=0).astype(jnp.bfloat16)
    for h in range(2):
        cols = slice(h * 256, (h + 1) * 256)
        owner = owners(owner_ref, 2 * h, 2)
        near = dot(pick, owner)
        parts = []
        for j in range(OWN):
            both = dot(left, one_hot(owner, base + j))
            parts.append(both[:ROWS] + both[ROWS:])
            fam = (base + j).astype(jnp.float32)
            u_ref[j * ROWS : (j + 1) * ROWS, cols] = jnp.where(near == fam, fidelity, 0.0)
        mixed = jnp.concatenate(parts, axis=0)
        upper = mixed.astype(jnp.bfloat16)
        x_ref[:, cols] = upper
        xl_ref[:, cols] = (mixed - upper.astype(jnp.float32)).astype(jnp.bfloat16)
    x, xl = x_ref[...], xl_ref[...]
    u_ref[...] = u_ref[...] + (dot(x, high) + dot(x, low) + dot(xl, high))


def sweep_kernel(u_ref, keep_ref, got_ref, out_ref, best_ref):
    top, other = keep_ref[0], got_ref[0]
    second = jnp.maximum(jnp.minimum(top, other), jnp.maximum(keep_ref[1], got_ref[1]))
    top = jnp.maximum(top, other)
    for j in range(OWN):
        u = u_ref[j * ROWS : (j + 1) * ROWS, :]
        second = jnp.maximum(jnp.minimum(top, u), second)
        top = jnp.maximum(top, u)
    best_ref[0] = top
    best_ref[1] = second

    def family(j, carry):
        u = u_ref[pl.ds(pl.multiple_of(j * ROWS, 8), ROWS), :]
        phi = scale_factor * (u - jnp.where(u >= best_ref[0], best_ref[1], best_ref[0]))
        sign = phi * lax.rsqrt(phi * phi + 1.0)
        side = jnp.where(sign > 0, 1.0, -1.0)
        pull = step_size * sign
        for _ in range(SWEEPS):
            slope = None
            for axis, length in ((0, ROWS), (1, NY)):
                back = phi - pltpu.roll(phi, 1, axis)
                fore = pltpu.roll(back, length - 1, axis)
                steep = jnp.maximum(jnp.maximum(side * back, -(side * fore)), 0.0)
                slope = steep * steep if slope is None else slope + steep * steep
            grad = slope * lax.rsqrt(jnp.maximum(slope, 1e-30))
            phi = phi - pull * (grad - 1.0)
        out_ref[j, 0, :, :] = phi[HALO : HALO + SLAB, :]
        return carry

    lax.fori_loop(0, OWN, family, 0, unroll=2)


VMEM = pl.BlockSpec(memory_space=pltpu.VMEM)
ANY = pl.BlockSpec(memory_space=pl.ANY)


def call(kernel, name, ins, outs, scratch, room, cost=None):
    return pl.pallas_call(
        kernel,
        out_shape=outs,
        in_specs=ins,
        out_specs=jax.tree.map(lambda _: VMEM, outs),
        scratch_shapes=scratch,
        compiler_params=pltpu.CompilerParams(vmem_limit_bytes=room << 20),
        cost_estimate=cost,
        name=name,
    )


def body(labels, family_of_grain):
    f32, bf16 = jnp.float32, jnp.bfloat16
    shape = jax.ShapeDtypeStruct
    lines = lax.axis_size(LINES)
    owner = call(
        lookup_kernel,
        "lookup",
        [ANY, ANY],
        shape((lines, TILES, SLAB, 128), bf16),
        [
            pltpu.VMEM((SLAB, NY), jnp.int32),
            pltpu.VMEM((GRAINS // 128, 128), jnp.int32),
            pltpu.SemaphoreType.DMA((2,)),
        ],
        4,
    )(labels.reshape(SLAB, NY), family_of_grain.reshape(GRAINS // 128, 128))
    owner = lax.all_to_all(owner, LINES, split_axis=0, concat_axis=0, tiled=True)
    high, low = (jnp.asarray(part) for part in smoothing_operator(NX))
    keep, send = call(
        rank_kernel,
        "rank",
        [VMEM] * 3,
        (shape((2, ROWS, NY), f32), shape((2, ROWS, NY), f32)),
        [
            pltpu.VMEM((2 * ROWS, NX), jnp.float8_e4m3fn),
            pltpu.VMEM((ROWS, NY), f32),
            pltpu.VMEM((NX, NY), jnp.int8),
            pltpu.VMEM((HALF * ROWS, NY), bf16),
            pltpu.VMEM((2, ROWS, NY), f32),
            pltpu.VMEM((PART * ROWS, NY), f32),
            pltpu.VMEM((PART * ROWS, NY), f32),
        ],
        24,
    )(owner, high, low)
    got = lax.ppermute(send, "x", [(i, i ^ 1) for i in range(lax.axis_size("x"))])
    u = call(
        own_kernel,
        "own",
        [VMEM] * 3,
        shape((OWN * ROWS, NY), f32),
        [pltpu.VMEM((OWN * ROWS, NY), bf16), pltpu.VMEM((OWN * ROWS, NY), bf16)],
        8,
        pl.CostEstimate(flops=10**9, bytes_accessed=10**6, transcendentals=0),
    )(owner, high, low)
    return call(
        sweep_kernel,
        "sweep",
        [VMEM] * 3,
        shape((OWN, 1, SLAB, NY), f32),
        [pltpu.VMEM((2, ROWS, NY), f32)],
        8,
    )(u, keep, got)


def solution(mesh):
    fine = Mesh(mesh.devices.reshape(2, 8, 2, 8, SHARE), LINES + FAMS)
    return jax.shard_map(
        body,
        mesh=fine,
        in_specs=(P(None, LINES, None), P()),
        out_specs=P(FAMS, None, LINES, None),
        check_vma=False,
    )
```

```python
import functools

import jax
import jax.numpy as jnp
import numpy as np
from jax import lax
from jax.experimental import pallas as pl
from jax.experimental.pallas import tpu as pltpu
from jax.sharding import Mesh, PartitionSpec as P

F = 256
NX = 512
NY = 512
GRAINS = 2048
WIDTH = 2
SWEEPS = 3

fidelity = 0.25
scale_factor = 8.0
step_size = 0.5

SLAB = 16
HALO = 4
ROWS = SLAB + 2 * HALO
CORES = 2
WIDE = CORES * SLAB + 2 * HALO
OWN = 8
BATCH = 4
STEPS = (F - OWN) // BATCH // CORES
GROUP = 8
OTHERS = STEPS * BATCH
CHUNKS = (32, 32, 32, OTHERS - 96)
TILES = NY // 128
PAD = 8
SIDES = 2
LOWEST = -1e30
GAIN = 512.0
FINE = 32.0
LINES = ("ylo", "z", "core")
CHIPS = ("ylo", "z")
FAMS = ("x", "yhi")
PARTNERS = [(0, 1), (1, 0)]

dot = functools.partial(jnp.dot, preferred_element_type=jnp.float32)


def smoothing_operator(count):
    idx = np.arange(count, dtype=np.float32)
    angle = np.float32(2.0 * np.pi) * np.outer(idx, idx) / np.float32(count)
    angle = angle.astype(np.float64)
    cas = (np.cos(angle) + np.sin(angle)).astype(np.float32).astype(jnp.bfloat16).astype(np.float64)
    mirror = np.minimum(np.arange(count), count - np.arange(count)).astype(np.float64)
    gauss = np.exp(-2.0 * np.pi**2 * (WIDTH / 2.0) ** 2 * mirror**2 / count**2)
    full = (cas * gauss) @ cas / count
    high = full.astype(np.float32).astype(jnp.bfloat16)
    low = (full - high.astype(np.float64)).astype(np.float32).astype(jnp.bfloat16)
    return [part.reshape(count, TILES, 128).transpose(1, 0, 2) for part in (high, low)]


def lookup_kernel(labels_hbm, table_hbm, out_ref, labels_ref, table_ref, sems):
    copies = [
        pltpu.make_async_copy(labels_hbm, labels_ref, sems.at[0]),
        pltpu.make_async_copy(table_hbm, table_ref, sems.at[1]),
    ]
    for copy in copies:
        copy.start()
    for copy in copies:
        copy.wait()
    for c in range(TILES):
        for r in range(0, SLAB, 8):
            label = labels_ref[r : r + 8, c * 128 : (c + 1) * 128]
            lane = label & 127
            part = label >> 7
            owner = jnp.zeros((8, 128), jnp.int32)
            for k in range(GRAINS // 128):
                line = jnp.broadcast_to(table_ref[k : k + 1, :], (8, 128))
                owner = jnp.where(part == k, jnp.take_along_axis(line, lane, axis=1), owner)
            value = owner.astype(jnp.float32).astype(jnp.bfloat16)
            for p in range(c // (TILES // SIDES), out_ref.shape[0], CORES):
                out_ref[p, c % (TILES // SIDES), r : r + 8, :] = value


def blocks(ref):
    return jnp.concatenate([ref[c] for c in range(TILES)], axis=1)


def owners(owner_ref):
    return jnp.concatenate([owner_ref[:, c].reshape(NX, 128) for c in range(TILES // SIDES)], axis=1)


def selector(start, rows):
    row = lax.broadcasted_iota(jnp.int32, (rows, NX), 0)
    col = lax.broadcasted_iota(jnp.int32, (rows, NX), 1)
    return jnp.where(((row + (start + NX)) & (NX - 1)) == col, 1.0, 0.0).astype(jnp.bfloat16)


def batch_of(step):
    mine = lax.axis_index(FAMS) * (OWN // BATCH)
    turn = lax.axis_index("core") * STEPS + step
    return (turn + (turn >= mine).astype(jnp.int32) * (OWN // BATCH)) * BATCH


def first_mix_kernel(owner_ref, high_ref, low_ref, x_ref, near_ref, left_ref, id_ref):
    pick = selector(lax.axis_index(CHIPS) * (CORES * SLAB) - HALO, WIDE)
    left = (dot(pick, blocks(high_ref)) + dot(pick, blocks(low_ref))) * GAIN
    coarse = left.astype(jnp.float8_e4m3fn)
    fine = ((left - coarse.astype(jnp.float32)) * FINE).astype(jnp.float8_e4m3fn)
    left_ref[...] = jnp.concatenate([coarse, fine], axis=0)
    mix_kernel(owner_ref, left_ref, x_ref, near_ref, id_ref)


def mix_kernel(owner_ref, left_ref, x_ref, near_ref, id_ref):
    f8 = jnp.float8_e4m3fn
    one, zero = jnp.ones((), f8), jnp.zeros((), f8)
    owner = owners(owner_ref)
    pick = selector(lax.axis_index(CHIPS) * (CORES * SLAB) - HALO, WIDE)
    near_ref[...] = dot(pick, owner)
    id_ref[...] = (owner.astype(jnp.float32).astype(jnp.int32) - 128).astype(jnp.int8)

    def mix(first, batches):
        left = left_ref[...]
        ids = id_ref[...]
        parts = []
        for b in range(batches):
            base = batch_of(first + b) - 128
            for j in range(BATCH):
                both = dot(left, jnp.where(ids == (base + j).astype(jnp.int8), one, zero))
                parts.append(both[:WIDE] + both[WIDE:] * (1.0 / FINE))
        at = first * (BATCH * WIDE)
        at = at if isinstance(at, int) else pl.multiple_of(at, 16)
        x_ref[pl.ds(at, batches * BATCH * WIDE), :] = jnp.concatenate(parts, axis=0).astype(jnp.bfloat16)

    def step(g, carry):
        mix(g * GROUP, GROUP)
        return carry

    lax.fori_loop(0, STEPS // GROUP, step, 0)
    mix(STEPS // GROUP * GROUP, STEPS % GROUP)


def side_of(turn):
    core = lax.axis_index("core")
    side = core if turn == 0 else CORES - 1 - core
    return pl.ds(pl.multiple_of(side * (NY // SIDES), 128), NY // SIDES)


def rank_kernel(xa_ref, xb_ref, na_ref, nb_ref, high_ref, keep_ref, send_ref, near_ref, best_ref, *u_refs):
    core = lax.axis_index("core")
    best_ref[...] = jnp.full((2, WIDE, NY), LOWEST, jnp.float32)
    tables = []
    for turn, ref in enumerate((na_ref, nb_ref)):
        near_ref[:, side_of(turn)] = ref[...]
        tables.append(jnp.concatenate([high_ref[c, side_of(turn), :] for c in range(TILES)], axis=1))
    start = 0
    for turn, count in enumerate(CHUNKS):
        u_ref = u_refs[turn % 2]
        rows = slice(start * WIDE, (start + count) * WIDE)
        u_ref[0 : count * WIDE, :] = dot(xa_ref[rows, :], tables[0]) + dot(xb_ref[rows, :], tables[1])
        for c in range(TILES):
            cols = slice(c * 128, (c + 1) * 128)
            near = near_ref[:, cols]
            top, second = best_ref[0, :, cols], best_ref[1, :, cols]
            for j in range(count):
                index = start + j
                fam = (batch_of(index // BATCH) + index % BATCH).astype(jnp.float32)
                u = u_ref[j * WIDE : (j + 1) * WIDE, cols] + jnp.where(near == fam, fidelity * GAIN, 0.0)
                second = jnp.maximum(jnp.minimum(top, u), second)
                top = jnp.maximum(top, u)
            best_ref[0, :, cols] = top
            best_ref[1, :, cols] = second
        start += count
    for k in range(2):
        for ref, offset in ((keep_ref, core * SLAB), (send_ref, (CORES - 1 - core) * SLAB)):
            ref[k] = best_ref[k, pl.ds(pl.multiple_of(offset, 8), ROWS), :] * (1.0 / GAIN)


def own_kernel(oa_ref, ob_ref, high_ref, low_ref, u_ref, x_ref, xl_ref):
    base = lax.axis_index(FAMS) * OWN
    pick = selector(lax.axis_index(LINES) * SLAB - HALO, ROWS)
    high, low = blocks(high_ref), blocks(low_ref)
    left = jnp.concatenate([dot(pick, high), dot(pick, low)], axis=0).astype(jnp.bfloat16)
    one, zero = jnp.ones((), jnp.bfloat16), jnp.zeros((), jnp.bfloat16)
    for turn, owner_ref in enumerate((oa_ref, ob_ref)):
        cols = side_of(turn)
        owner = owners(owner_ref)
        near = dot(pick, owner)
        parts = []
        for j in range(OWN):
            fam = (base + j).astype(jnp.float32)
            both = dot(left, jnp.where(owner == fam.astype(jnp.bfloat16), one, zero))
            parts.append(both[:ROWS] + both[ROWS:])
            u_ref[j * ROWS : (j + 1) * ROWS, cols] = jnp.where(near == fam, fidelity, 0.0)
        mixed = jnp.concatenate(parts, axis=0)
        upper = mixed.astype(jnp.bfloat16)
        x_ref[:, cols] = upper
        xl_ref[:, cols] = (mixed - upper.astype(jnp.float32)).astype(jnp.bfloat16)
    x, xl = x_ref[...], xl_ref[...]
    u_ref[...] = u_ref[...] + (dot(x, high) + dot(x, low) + dot(xl, high))


def sweep_kernel(u_ref, keep_ref, got_ref, out_hbm, best_ref, phi_ref, pull_ref, done_ref, sems):
    top, other = keep_ref[0], got_ref[0]
    second = jnp.maximum(jnp.minimum(top, other), jnp.maximum(keep_ref[1], got_ref[1]))
    top = jnp.maximum(top, other)
    for j in range(OWN):
        u = u_ref[j * ROWS : (j + 1) * ROWS, :]
        second = jnp.maximum(jnp.minimum(top, u), second)
        top = jnp.maximum(top, u)
    best_ref[0] = top
    best_ref[1] = second
    phi_ref[...] = jnp.zeros(phi_ref.shape, jnp.float32)
    lane = lax.broadcasted_iota(jnp.int32, (ROWS, 128), 1)
    begins, ends = lane == 0, lane == 127

    def pair(i, carry):
        fams = [2 * i + n for n in range(2)]
        state = {}
        for n, j in enumerate(fams):
            at = pl.multiple_of(j * ROWS, 8)
            for c in range(TILES):
                cols = slice(c * 128, (c + 1) * 128)
                u = u_ref[pl.ds(at, ROWS), cols]
                top = best_ref[0, :, cols]
                phi = scale_factor * (u - jnp.where(u >= top, best_ref[1, :, cols], top))
                pull_ref[n, c] = (step_size * phi) * lax.rsqrt(phi * phi + 1.0)
                state[n, c] = phi
        for _ in range(SWEEPS):
            after, ahead = {}, {}
            for key, phi in state.items():
                phi_ref[key[0], key[1], PAD : PAD + ROWS, :] = phi
                after[key] = pltpu.roll(phi, 1, 1)
                ahead[key] = pltpu.roll(phi, 127, 1)
            for (n, c), phi in list(state.items()):
                pull = pull_ref[n, c]
                side = jnp.where(pull > 0, 1.0, -1.0)
                slope = None
                for low, high in (
                    (
                        phi_ref[n, c, PAD - 1 : PAD - 1 + ROWS, :],
                        phi_ref[n, c, PAD + 1 : PAD + 1 + ROWS, :],
                    ),
                    (
                        jnp.where(begins, after[n, (c - 1) % TILES], after[n, c]),
                        jnp.where(ends, ahead[n, (c + 1) % TILES], ahead[n, c]),
                    ),
                ):
                    steep = jnp.maximum(jnp.maximum(side * (phi - low), side * (phi - high)), 0.0)
                    slope = steep * steep if slope is None else slope + steep * steep
                grad = slope * lax.rsqrt(jnp.maximum(slope, 1e-30))
                state[n, c] = phi - pull * (grad - 1.0)
        for n, j in enumerate(fams):
            for c in range(TILES):
                phi_ref[n, c, PAD : PAD + ROWS, :] = state[n, c]
                done_ref[j, 0, :, c * 128 : (c + 1) * 128] = phi_ref[n, c, PAD + HALO : PAD + HALO + SLAB, :]
            pltpu.make_async_copy(done_ref.at[j], out_hbm.at[j], sems.at[j]).start()
        return carry

    lax.fori_loop(0, OWN // 2, pair, 0)
    for j in range(OWN):
        pltpu.make_async_copy(done_ref.at[j], out_hbm.at[j], sems.at[j]).wait()


VMEM = pl.BlockSpec(memory_space=pltpu.VMEM)
HBM = pl.BlockSpec(memory_space=pltpu.HBM)


def cost(flops):
    return pl.CostEstimate(flops=flops, bytes_accessed=10**6, transcendentals=0)


def call(kernel, name, ins, outs, scratch, room, estimate=None, where=None):
    return pl.pallas_call(
        kernel,
        out_shape=outs,
        in_specs=ins,
        out_specs=jax.tree.map(lambda _: VMEM, outs) if where is None else where,
        scratch_shapes=scratch,
        compiler_params=pltpu.CompilerParams(vmem_limit_bytes=room << 20),
        cost_estimate=estimate,
        name=name,
    )


def body(labels, family_of_grain):
    f32, bf16 = jnp.float32, jnp.bfloat16
    shape = jax.ShapeDtypeStruct
    lines = lax.axis_size(LINES)
    high, low = (jnp.asarray(part) for part in smoothing_operator(NX))
    owner = call(
        lookup_kernel,
        "lookup",
        [HBM, HBM],
        shape((lines, TILES // SIDES, SLAB, 128), bf16),
        [
            pltpu.VMEM((SLAB, NY), jnp.int32),
            pltpu.VMEM((GRAINS // 128, 128), jnp.int32),
            pltpu.SemaphoreType.DMA((2,)),
        ],
        4,
    )(labels.reshape(SLAB, NY), family_of_grain.reshape(GRAINS // 128, 128))
    owner = lax.all_to_all(owner, LINES, split_axis=0, concat_axis=0, tiled=True)
    sides = [owner, lax.ppermute(owner, "core", PARTNERS)]
    mixed = (shape((OTHERS * WIDE, NY // SIDES), bf16), shape((WIDE, NY // SIDES), f32))
    ids = [pltpu.VMEM((NX, NY // SIDES), jnp.int8)]
    xa, na, left = call(
        first_mix_kernel,
        "mix_first",
        [VMEM] * 3,
        mixed + (shape((2 * WIDE, NX), jnp.float8_e4m3fn),),
        ids,
        8,
        cost(10**9),
    )(sides[0], high, low)
    xb, nb = call(mix_kernel, "mix_second", [VMEM] * 2, mixed, ids, 8, cost(10**9))(sides[1], left)
    keep, send = call(
        rank_kernel,
        "rank",
        [VMEM] * 5,
        (shape((2, ROWS, NY), f32), shape((2, ROWS, NY), f32)),
        [pltpu.VMEM((WIDE, NY), f32), pltpu.VMEM((2, WIDE, NY), f32)]
        + [pltpu.VMEM((max(CHUNKS) * WIDE, NY), f32)] * 2,
        16,
    )(xa, xb, na, nb, high)
    got = lax.ppermute(send, "core", PARTNERS)
    u = call(
        own_kernel,
        "own",
        [VMEM] * 4,
        shape((OWN * ROWS, NY), f32),
        [pltpu.VMEM((OWN * ROWS, NY), bf16), pltpu.VMEM((OWN * ROWS, NY), bf16)],
        8,
        cost(10**9),
    )(*sides, high, low)
    return call(
        sweep_kernel,
        "sweep",
        [VMEM] * 3,
        shape((OWN, 1, SLAB, NY), f32),
        [
            pltpu.VMEM((2, ROWS, NY), f32),
            pltpu.VMEM((2, TILES, PAD + ROWS + 8, 128), f32),
            pltpu.VMEM((2, TILES, ROWS, 128), f32),
            pltpu.VMEM((OWN, 1, SLAB, NY), f32),
            pltpu.SemaphoreType.DMA((OWN,)),
        ],
        8,
        where=HBM,
    )(u, keep, got)


def solution(mesh):
    fine = Mesh(mesh.devices.reshape(2, 8, CORES, 8, 4), LINES + FAMS)
    return jax.shard_map(
        body,
        mesh=fine,
        in_specs=(P(None, LINES, None), P()),
        out_specs=P(FAMS, None, LINES, None),
        check_vma=False,
    )
```

```python
import functools

import jax
import jax.numpy as jnp
import numpy as np
from jax import lax
from jax.experimental import pallas as pl
from jax.experimental.pallas import tpu as pltpu
from jax.sharding import Mesh, PartitionSpec as P

F = 256
NX = 512
NY = 512
GRAINS = 2048
WIDTH = 2
SWEEPS = 3

fidelity = 0.25
scale_factor = 8.0
step_size = 0.5

SLAB = 16
HALO = 4
ROWS = SLAB + 2 * HALO
CORES = 2
WIDE = CORES * SLAB + 2 * HALO
OWN = 8
BATCH = 4
STEPS = (F - OWN) // BATCH // CORES
GROUP = 31
OTHERS = STEPS * BATCH
CHUNKS = (32, 32, 32, OTHERS - 96)
TILES = NY // 128
PAD = 8
SIDES = 2
LOWEST = -1e30
GAIN = 512.0
FINE = 32.0
LINES = ("ylo", "z", "core")
CHIPS = ("ylo", "z")
FAMS = ("x", "yhi")
PARTNERS = [(0, 1), (1, 0)]

dot = functools.partial(jnp.dot, preferred_element_type=jnp.float32)


def smoothing_operator(count):
    idx = np.arange(count, dtype=np.float32)
    angle = np.float32(2.0 * np.pi) * np.outer(idx, idx) / np.float32(count)
    angle = angle.astype(np.float64)
    cas = (np.cos(angle) + np.sin(angle)).astype(np.float32).astype(jnp.bfloat16).astype(np.float64)
    mirror = np.minimum(np.arange(count), count - np.arange(count)).astype(np.float64)
    gauss = np.exp(-2.0 * np.pi**2 * (WIDTH / 2.0) ** 2 * mirror**2 / count**2)
    full = (cas * gauss) @ cas / count
    high = full.astype(np.float32).astype(jnp.bfloat16)
    low = (full - high.astype(np.float64)).astype(np.float32).astype(jnp.bfloat16)
    return [part.reshape(count, TILES, 128).transpose(1, 0, 2) for part in (high, low)]


def mixing_rows(high, low, chips):
    f8 = jnp.float8_e4m3fn
    full = (high.astype(np.float64) + low.astype(np.float64)).transpose(1, 0, 2).reshape(NX, NX) * GAIN
    full = full.astype(np.float32)
    coarse = full.astype(f8)
    fine = ((full - coarse.astype(np.float32)) * np.float32(FINE)).astype(f8)
    rows = (np.arange(chips)[:, None] * (CORES * SLAB) - HALO + np.arange(WIDE)[None]) % NX
    return np.concatenate([coarse[rows], fine[rows]], axis=1)


def lookup_kernel(labels_hbm, table_hbm, rows_hbm, out_ref, left_ref, labels_ref, table_ref, sems):
    copies = [
        pltpu.make_async_copy(labels_hbm, labels_ref, sems.at[0]),
        pltpu.make_async_copy(table_hbm, table_ref, sems.at[1]),
        pltpu.make_async_copy(rows_hbm.at[lax.axis_index(CHIPS)], left_ref, sems.at[2]),
    ]
    for copy in copies:
        copy.start()
    for copy in copies[:2]:
        copy.wait()
    for c in range(TILES):
        for r in range(0, SLAB, 8):
            label = labels_ref[r : r + 8, c * 128 : (c + 1) * 128]
            lane = label & 127
            part = label >> 7
            owner = jnp.zeros((8, 128), jnp.int32)
            for k in range(GRAINS // 128):
                line = jnp.broadcast_to(table_ref[k : k + 1, :], (8, 128))
                owner = jnp.where(part == k, jnp.take_along_axis(line, lane, axis=1), owner)
            value = owner.astype(jnp.float32).astype(jnp.bfloat16)
            for p in range(c // (TILES // SIDES), out_ref.shape[0], CORES):
                out_ref[p, c % (TILES // SIDES), r : r + 8, :] = value
    copies[2].wait()


def blocks(ref):
    return jnp.concatenate([ref[c] for c in range(TILES)], axis=1)


def owners(owner_ref):
    return jnp.concatenate([owner_ref[:, c].reshape(NX, 128) for c in range(TILES // SIDES)], axis=1)


def selector(start, rows):
    row = lax.broadcasted_iota(jnp.int32, (rows, NX), 0)
    col = lax.broadcasted_iota(jnp.int32, (rows, NX), 1)
    return jnp.where(((row + (start + NX)) & (NX - 1)) == col, 1.0, 0.0).astype(jnp.bfloat16)


def batch_of(step):
    mine = lax.axis_index(FAMS) * (OWN // BATCH)
    turn = lax.axis_index("core") * STEPS + step
    return (turn + (turn >= mine).astype(jnp.int32) * (OWN // BATCH)) * BATCH


def mix_kernel(owner_ref, left_ref, x_ref, near_ref, id_ref):
    f8 = jnp.float8_e4m3fn
    one, zero = jnp.ones((), f8), jnp.zeros((), f8)
    owner = owners(owner_ref)
    pick = selector(lax.axis_index(CHIPS) * (CORES * SLAB) - HALO, WIDE)
    near_ref[...] = dot(pick, owner)
    id_ref[...] = (owner.astype(jnp.float32).astype(jnp.int32) - 128).astype(jnp.int8)

    def mix(first, batches):
        left = left_ref[...]
        ids = id_ref[...]
        parts = []
        for b in range(batches):
            base = batch_of(first + b) - 128
            for j in range(BATCH):
                both = dot(left, jnp.where(ids == (base + j).astype(jnp.int8), one, zero))
                parts.append(both[:WIDE] + both[WIDE:] * (1.0 / FINE))
        at = first * (BATCH * WIDE)
        at = at if isinstance(at, int) else pl.multiple_of(at, 16)
        x_ref[pl.ds(at, batches * BATCH * WIDE), :] = jnp.concatenate(parts, axis=0).astype(jnp.bfloat16)

    def step(g, carry):
        mix(g * GROUP, GROUP)
        return carry

    lax.fori_loop(0, STEPS // GROUP, step, 0)
    if STEPS % GROUP:
        mix(STEPS // GROUP * GROUP, STEPS % GROUP)


def side_of(turn):
    core = lax.axis_index("core")
    side = core if turn == 0 else CORES - 1 - core
    return pl.ds(pl.multiple_of(side * (NY // SIDES), 128), NY // SIDES)


def rank_kernel(xa_ref, xb_ref, na_ref, nb_ref, high_ref, keep_ref, send_ref, near_ref, best_ref, *u_refs):
    core = lax.axis_index("core")
    best_ref[...] = jnp.full((2, WIDE, NY), LOWEST, jnp.float32)
    tables = []
    for turn, ref in enumerate((na_ref, nb_ref)):
        near_ref[:, side_of(turn)] = ref[...]
        tables.append(jnp.concatenate([high_ref[c, side_of(turn), :] for c in range(TILES)], axis=1))
    start = 0
    for turn, count in enumerate(CHUNKS):
        u_ref = u_refs[turn % 2]
        rows = slice(start * WIDE, (start + count) * WIDE)
        u_ref[0 : count * WIDE, :] = dot(xa_ref[rows, :], tables[0]) + dot(xb_ref[rows, :], tables[1])
        for c in range(TILES):
            cols = slice(c * 128, (c + 1) * 128)
            near = near_ref[:, cols]
            top, second = best_ref[0, :, cols], best_ref[1, :, cols]
            for j in range(count):
                index = start + j
                fam = (batch_of(index // BATCH) + index % BATCH).astype(jnp.float32)
                u = u_ref[j * WIDE : (j + 1) * WIDE, cols] + jnp.where(near == fam, fidelity * GAIN, 0.0)
                second = jnp.maximum(jnp.minimum(top, u), second)
                top = jnp.maximum(top, u)
            best_ref[0, :, cols] = top
            best_ref[1, :, cols] = second
        start += count
    for k in range(2):
        for ref, offset in ((keep_ref, core * SLAB), (send_ref, (CORES - 1 - core) * SLAB)):
            ref[k] = best_ref[k, pl.ds(pl.multiple_of(offset, 8), ROWS), :] * (1.0 / GAIN)


def own_kernel(oa_ref, ob_ref, high_ref, low_ref, u_ref, x_ref, xl_ref):
    base = lax.axis_index(FAMS) * OWN
    pick = selector(lax.axis_index(LINES) * SLAB - HALO, ROWS)
    high, low = blocks(high_ref), blocks(low_ref)
    left = jnp.concatenate([dot(pick, high), dot(pick, low)], axis=0).astype(jnp.bfloat16)
    one, zero = jnp.ones((), jnp.bfloat16), jnp.zeros((), jnp.bfloat16)
    for turn, owner_ref in enumerate((oa_ref, ob_ref)):
        cols = side_of(turn)
        owner = owners(owner_ref)
        near = dot(pick, owner)
        parts = []
        for j in range(OWN):
            fam = (base + j).astype(jnp.float32)
            both = dot(left, jnp.where(owner == fam.astype(jnp.bfloat16), one, zero))
            parts.append(both[:ROWS] + both[ROWS:])
            u_ref[j * ROWS : (j + 1) * ROWS, cols] = jnp.where(near == fam, fidelity, 0.0)
        mixed = jnp.concatenate(parts, axis=0)
        upper = mixed.astype(jnp.bfloat16)
        x_ref[:, cols] = upper
        xl_ref[:, cols] = (mixed - upper.astype(jnp.float32)).astype(jnp.bfloat16)
    x, xl = x_ref[...], xl_ref[...]
    u_ref[...] = u_ref[...] + (dot(x, high) + dot(x, low) + dot(xl, high))


def sweep_kernel(u_ref, keep_ref, got_ref, out_hbm, best_ref, phi_ref, pull_ref, side_ref, done_ref, sems):
    top, other = keep_ref[0], got_ref[0]
    second = jnp.maximum(jnp.minimum(top, other), jnp.maximum(keep_ref[1], got_ref[1]))
    top = jnp.maximum(top, other)
    for j in range(OWN):
        u = u_ref[j * ROWS : (j + 1) * ROWS, :]
        second = jnp.maximum(jnp.minimum(top, u), second)
        top = jnp.maximum(top, u)
    best_ref[0] = top
    best_ref[1] = second
    phi_ref[...] = jnp.zeros(phi_ref.shape, jnp.float32)
    lane = lax.broadcasted_iota(jnp.int32, (ROWS, 128), 1)
    begins, ends = lane == 0, lane == 127

    def pair(i, carry):
        fams = [2 * i + n for n in range(2)]
        state = {}
        for n, j in enumerate(fams):
            at = pl.multiple_of(j * ROWS, 8)
            for c in range(TILES):
                cols = slice(c * 128, (c + 1) * 128)
                u = u_ref[pl.ds(at, ROWS), cols]
                top = best_ref[0, :, cols]
                phi = scale_factor * (u - jnp.where(u >= top, best_ref[1, :, cols], top))
                pull_ref[n, c] = (step_size * phi) * lax.rsqrt(phi * phi + 1.0)
                side_ref[n, c] = jnp.where(phi > 0, 1.0, -1.0)
                state[n, c] = phi
        for _ in range(SWEEPS):
            after, ahead = {}, {}
            for key, phi in state.items():
                phi_ref[key[0], key[1], PAD : PAD + ROWS, :] = phi
                after[key] = pltpu.roll(phi, 1, 1)
                ahead[key] = pltpu.roll(phi, 127, 1)
            for (n, c), phi in list(state.items()):
                pull = pull_ref[n, c]
                side = side_ref[n, c]
                slope = None
                for low, high in (
                    (
                        phi_ref[n, c, PAD - 1 : PAD - 1 + ROWS, :],
                        phi_ref[n, c, PAD + 1 : PAD + 1 + ROWS, :],
                    ),
                    (
                        jnp.where(begins, after[n, (c - 1) % TILES], after[n, c]),
                        jnp.where(ends, ahead[n, (c + 1) % TILES], ahead[n, c]),
                    ),
                ):
                    steep = jnp.maximum(jnp.maximum(side * (phi - low), side * (phi - high)), 0.0)
                    slope = steep * steep if slope is None else slope + steep * steep
                grad = slope * lax.rsqrt(jnp.maximum(slope, 1e-30))
                state[n, c] = phi - pull * (grad - 1.0)
        for n, j in enumerate(fams):
            for c in range(TILES):
                phi_ref[n, c, PAD : PAD + ROWS, :] = state[n, c]
                done_ref[j, 0, :, c * 128 : (c + 1) * 128] = phi_ref[n, c, PAD + HALO : PAD + HALO + SLAB, :]
            pltpu.make_async_copy(done_ref.at[j], out_hbm.at[j], sems.at[j]).start()
        return carry

    lax.fori_loop(0, OWN // 2, pair, 0)
    for j in range(OWN):
        pltpu.make_async_copy(done_ref.at[j], out_hbm.at[j], sems.at[j]).wait()


VMEM = pl.BlockSpec(memory_space=pltpu.VMEM)
HBM = pl.BlockSpec(memory_space=pltpu.HBM)


def pinned(array):
    return pltpu.with_memory_space_constraint(array, pltpu.HBM)


def cost(flops):
    return pl.CostEstimate(flops=flops, bytes_accessed=10**6, transcendentals=0)


def call(kernel, name, ins, outs, scratch, room, estimate=None, where=None):
    return pl.pallas_call(
        kernel,
        out_shape=outs,
        in_specs=ins,
        out_specs=jax.tree.map(lambda _: VMEM, outs) if where is None else where,
        scratch_shapes=scratch,
        compiler_params=pltpu.CompilerParams(vmem_limit_bytes=room << 20),
        cost_estimate=estimate,
        name=name,
    )


def body(labels, family_of_grain):
    f32, bf16 = jnp.float32, jnp.bfloat16
    shape = jax.ShapeDtypeStruct
    lines = lax.axis_size(LINES)
    tables = smoothing_operator(NX)
    rows = jnp.asarray(mixing_rows(*tables, lax.axis_size(CHIPS)))
    high, low = (jnp.asarray(part) for part in tables)
    owner, left = call(
        lookup_kernel,
        "lookup",
        [HBM] * 3,
        (
            shape((lines, TILES // SIDES, SLAB, 128), bf16),
            shape((2 * WIDE, NX), jnp.float8_e4m3fn),
        ),
        [
            pltpu.VMEM((SLAB, NY), jnp.int32),
            pltpu.VMEM((GRAINS // 128, 128), jnp.int32),
            pltpu.SemaphoreType.DMA((3,)),
        ],
        4,
    )(
        pinned(labels.reshape(SLAB, NY)),
        pinned(family_of_grain.reshape(GRAINS // 128, 128)),
        pinned(rows),
    )
    owner = lax.all_to_all(owner, LINES, split_axis=0, concat_axis=0, tiled=True)
    sides = [owner, lax.ppermute(owner, "core", PARTNERS)]
    mixed = (shape((OTHERS * WIDE, NY // SIDES), bf16), shape((WIDE, NY // SIDES), f32))
    ids = [pltpu.VMEM((NX, NY // SIDES), jnp.int8)]
    (xa, na), (xb, nb) = (
        call(mix_kernel, "mix", [VMEM] * 2, mixed, ids, 8, cost(10**9))(side, left) for side in sides
    )
    keep, send = call(
        rank_kernel,
        "rank",
        [VMEM] * 5,
        (shape((2, ROWS, NY), f32), shape((2, ROWS, NY), f32)),
        [pltpu.VMEM((WIDE, NY), f32), pltpu.VMEM((2, WIDE, NY), f32)]
        + [pltpu.VMEM((max(CHUNKS) * WIDE, NY), f32)] * 2,
        16,
    )(xa, xb, na, nb, high)
    got = lax.ppermute(send, "core", PARTNERS)
    u = call(
        own_kernel,
        "own",
        [VMEM] * 4,
        shape((OWN * ROWS, NY), f32),
        [pltpu.VMEM((OWN * ROWS, NY), bf16), pltpu.VMEM((OWN * ROWS, NY), bf16)],
        8,
        cost(10**9),
    )(*sides, high, low)
    return call(
        sweep_kernel,
        "sweep",
        [VMEM] * 3,
        shape((OWN, 1, SLAB, NY), f32),
        [
            pltpu.VMEM((2, ROWS, NY), f32),
            pltpu.VMEM((2, TILES, PAD + ROWS + 8, 128), f32),
            pltpu.VMEM((2, TILES, ROWS, 128), f32),
            pltpu.VMEM((2, TILES, ROWS, 128), f32),
            pltpu.VMEM((OWN, 1, SLAB, NY), f32),
            pltpu.SemaphoreType.DMA((OWN,)),
        ],
        8,
        where=HBM,
    )(u, keep, got)


def solution(mesh):
    fine = Mesh(mesh.devices.reshape(2, 8, CORES, 8, 4), LINES + FAMS)
    return jax.shard_map(
        body,
        mesh=fine,
        in_specs=(P(None, LINES, None), P()),
        out_specs=P(FAMS, None, LINES, None),
        check_vma=False,
    )
```

```python
import functools

import jax
import jax.numpy as jnp
import numpy as np
from jax import lax
from jax.experimental import pallas as pl
from jax.experimental.pallas import tpu as pltpu
from jax.sharding import Mesh, PartitionSpec as P

F = 256
NX = 512
NY = 512
GRAINS = 2048
WIDTH = 2
SWEEPS = 3

fidelity = 0.25
scale_factor = 8.0
step_size = 0.5

SLAB = 16
HALO = 4
ROWS = SLAB + 2 * HALO
CORES = 2
WIDE = CORES * SLAB + 2 * HALO
OWN = 8
BATCH = 4
STEPS = (F - OWN) // BATCH // CORES
GROUP = 31
OTHERS = STEPS * BATCH
CHUNKS = (12,) * 10 + (OTHERS - 120,)
TILES = NY // 128
PAD = 8
SIDES = 2
LOWEST = -1e30
GAIN = 512.0
FINE = 32.0
LINES = ("ylo", "z", "core")
CHIPS = ("ylo", "z")
FAMS = ("x", "yhi")
PARTNERS = [(0, 1), (1, 0)]

dot = functools.partial(jnp.dot, preferred_element_type=jnp.float32)


def smoothing_operator(count):
    idx = np.arange(count, dtype=np.float32)
    angle = np.float32(2.0 * np.pi) * np.outer(idx, idx) / np.float32(count)
    angle = angle.astype(np.float64)
    cas = (np.cos(angle) + np.sin(angle)).astype(np.float32).astype(jnp.bfloat16).astype(np.float64)
    mirror = np.minimum(np.arange(count), count - np.arange(count)).astype(np.float64)
    gauss = np.exp(-2.0 * np.pi**2 * (WIDTH / 2.0) ** 2 * mirror**2 / count**2)
    full = (cas * gauss) @ cas / count
    high = full.astype(np.float32).astype(jnp.bfloat16)
    low = (full - high.astype(np.float64)).astype(np.float32).astype(jnp.bfloat16)
    return [part.reshape(count, TILES, 128).transpose(1, 0, 2) for part in (high, low)]


def mixing_rows(high, low, chips):
    f8 = jnp.float8_e4m3fn
    full = (high.astype(np.float64) + low.astype(np.float64)).transpose(1, 0, 2).reshape(NX, NX) * GAIN
    full = full.astype(np.float32)
    coarse = full.astype(f8)
    fine = ((full - coarse.astype(np.float32)) * np.float32(FINE)).astype(f8)
    rows = (np.arange(chips)[:, None] * (CORES * SLAB) - HALO + np.arange(WIDE)[None]) % NX
    return np.concatenate([coarse[rows], fine[rows]], axis=1)


def lookup_kernel(labels_hbm, table_hbm, rows_hbm, out_ref, left_ref, labels_ref, table_ref, sems):
    copies = [
        pltpu.make_async_copy(labels_hbm, labels_ref, sems.at[0]),
        pltpu.make_async_copy(table_hbm, table_ref, sems.at[1]),
        pltpu.make_async_copy(rows_hbm.at[lax.axis_index(CHIPS)], left_ref, sems.at[2]),
    ]
    for copy in copies:
        copy.start()
    for copy in copies[:2]:
        copy.wait()
    for c in range(TILES):
        for r in range(0, SLAB, 8):
            label = labels_ref[r : r + 8, c * 128 : (c + 1) * 128]
            lane = label & 127
            part = label >> 7
            owner = jnp.zeros((8, 128), jnp.int32)
            for k in range(GRAINS // 128):
                line = jnp.broadcast_to(table_ref[k : k + 1, :], (8, 128))
                owner = jnp.where(part == k, jnp.take_along_axis(line, lane, axis=1), owner)
            value = owner.astype(jnp.float32).astype(jnp.bfloat16)
            for p in range(c // (TILES // SIDES), out_ref.shape[0], CORES):
                out_ref[p, c % (TILES // SIDES), r : r + 8, :] = value
    copies[2].wait()


def blocks(ref):
    return jnp.concatenate([ref[c] for c in range(TILES)], axis=1)


def owners(owner_ref):
    return jnp.concatenate([owner_ref[:, c].reshape(NX, 128) for c in range(TILES // SIDES)], axis=1)


def selector(start, rows):
    row = lax.broadcasted_iota(jnp.int32, (rows, NX), 0)
    col = lax.broadcasted_iota(jnp.int32, (rows, NX), 1)
    return jnp.where(((row + (start + NX)) & (NX - 1)) == col, 1.0, 0.0).astype(jnp.bfloat16)


def batch_of(step):
    mine = lax.axis_index(FAMS) * (OWN // BATCH)
    turn = lax.axis_index("core") * STEPS + step
    return (turn + (turn >= mine).astype(jnp.int32) * (OWN // BATCH)) * BATCH


def mix_kernel(owner_ref, left_ref, x_ref, near_ref, id_ref):
    f8 = jnp.float8_e4m3fn
    one, zero = jnp.ones((), f8), jnp.zeros((), f8)
    owner = owners(owner_ref)
    pick = selector(lax.axis_index(CHIPS) * (CORES * SLAB) - HALO, WIDE)
    near_ref[...] = dot(pick, owner)
    id_ref[...] = (owner.astype(jnp.float32).astype(jnp.int32) - 128).astype(jnp.int8)

    def mix(first, batches):
        left = left_ref[...]
        ids = id_ref[...]
        parts = []
        for b in range(batches):
            base = batch_of(first + b) - 128
            for j in range(BATCH):
                both = dot(left, jnp.where(ids == (base + j).astype(jnp.int8), one, zero))
                parts.append(both[:WIDE] + both[WIDE:] * (1.0 / FINE))
        at = first * (BATCH * WIDE)
        at = at if isinstance(at, int) else pl.multiple_of(at, 16)
        x_ref[pl.ds(at, batches * BATCH * WIDE), :] = jnp.concatenate(parts, axis=0).astype(jnp.bfloat16)

    def step(g, carry):
        mix(g * GROUP, GROUP)
        return carry

    lax.fori_loop(0, STEPS // GROUP, step, 0)
    if STEPS % GROUP:
        mix(STEPS // GROUP * GROUP, STEPS % GROUP)


def side_of(turn):
    core = lax.axis_index("core")
    side = core if turn == 0 else CORES - 1 - core
    return pl.ds(pl.multiple_of(side * (NY // SIDES), 128), NY // SIDES)


def rank_kernel(xa_ref, xb_ref, na_ref, nb_ref, high_ref, keep_ref, send_ref, near_ref, best_ref, *u_refs):
    core = lax.axis_index("core")
    best_ref[...] = jnp.full((2, WIDE, NY), LOWEST, jnp.float32)
    tables = []
    for turn, ref in enumerate((na_ref, nb_ref)):
        near_ref[:, side_of(turn)] = ref[...]
        tables.append(jnp.concatenate([high_ref[c, side_of(turn), :] for c in range(TILES)], axis=1))
    start = 0
    for turn, count in enumerate(CHUNKS):
        u_ref = u_refs[turn % 2]
        rows = slice(start * WIDE, (start + count) * WIDE)
        u_ref[0 : count * WIDE, :] = dot(xa_ref[rows, :], tables[0]) + dot(xb_ref[rows, :], tables[1])
        for c in range(TILES):
            cols = slice(c * 128, (c + 1) * 128)
            near = near_ref[:, cols]
            top, second = best_ref[0, :, cols], best_ref[1, :, cols]
            for j in range(count):
                index = start + j
                fam = (batch_of(index // BATCH) + index % BATCH).astype(jnp.float32)
                u = u_ref[j * WIDE : (j + 1) * WIDE, cols] + jnp.where(near == fam, fidelity * GAIN, 0.0)
                second = jnp.maximum(jnp.minimum(top, u), second)
                top = jnp.maximum(top, u)
            best_ref[0, :, cols] = top
            best_ref[1, :, cols] = second
        start += count
    for k in range(2):
        for ref, offset in ((keep_ref, core * SLAB), (send_ref, (CORES - 1 - core) * SLAB)):
            ref[k] = best_ref[k, pl.ds(pl.multiple_of(offset, 8), ROWS), :] * (1.0 / GAIN)


def own_kernel(oa_ref, ob_ref, high_ref, low_ref, u_ref, x_ref, xl_ref):
    base = lax.axis_index(FAMS) * OWN
    pick = selector(lax.axis_index(LINES) * SLAB - HALO, ROWS)
    high, low = blocks(high_ref), blocks(low_ref)
    left = jnp.concatenate([dot(pick, high), dot(pick, low)], axis=0).astype(jnp.bfloat16)
    one, zero = jnp.ones((), jnp.bfloat16), jnp.zeros((), jnp.bfloat16)
    for turn, owner_ref in enumerate((oa_ref, ob_ref)):
        cols = side_of(turn)
        owner = owners(owner_ref)
        near = dot(pick, owner)
        parts = []
        for j in range(OWN):
            fam = (base + j).astype(jnp.float32)
            both = dot(left, jnp.where(owner == fam.astype(jnp.bfloat16), one, zero))
            parts.append(both[:ROWS] + both[ROWS:])
            u_ref[j * ROWS : (j + 1) * ROWS, cols] = jnp.where(near == fam, fidelity, 0.0)
        mixed = jnp.concatenate(parts, axis=0)
        upper = mixed.astype(jnp.bfloat16)
        x_ref[:, cols] = upper
        xl_ref[:, cols] = (mixed - upper.astype(jnp.float32)).astype(jnp.bfloat16)
    x, xl = x_ref[...], xl_ref[...]
    u_ref[...] = u_ref[...] + (dot(x, high) + dot(x, low) + dot(xl, high))


def sweep_kernel(u_ref, keep_ref, got_ref, out_hbm, best_ref, phi_ref, pull_ref, side_ref, done_ref, sems):
    top, other = keep_ref[0], got_ref[0]
    second = jnp.maximum(jnp.minimum(top, other), jnp.maximum(keep_ref[1], got_ref[1]))
    top = jnp.maximum(top, other)
    for j in range(OWN):
        u = u_ref[j * ROWS : (j + 1) * ROWS, :]
        second = jnp.maximum(jnp.minimum(top, u), second)
        top = jnp.maximum(top, u)
    best_ref[0] = top
    best_ref[1] = second
    phi_ref[...] = jnp.zeros(phi_ref.shape, jnp.float32)
    lane = lax.broadcasted_iota(jnp.int32, (ROWS, 128), 1)
    begins, ends = lane == 0, lane == 127

    def pair(i, carry):
        fams = [2 * i + n for n in range(2)]
        state = {}
        for n, j in enumerate(fams):
            for c in range(TILES):
                cols = slice(c * 128, (c + 1) * 128)
                u = u_ref[j * ROWS : (j + 1) * ROWS, cols]
                top = best_ref[0, :, cols]
                phi = scale_factor * (u - jnp.where(u >= top, best_ref[1, :, cols], top))
                pull_ref[2 * (i % 2) + n, c] = (step_size * phi) * lax.rsqrt(phi * phi + 1.0)
                side_ref[2 * (i % 2) + n, c] = jnp.where(phi > 0, 1.0, -1.0)
                state[n, c] = phi
        for _ in range(SWEEPS):
            after, ahead = {}, {}
            for key, phi in state.items():
                phi_ref[2 * (i % 2) + key[0], key[1], PAD : PAD + ROWS, :] = phi
                after[key] = pltpu.roll(phi, 1, 1)
                ahead[key] = pltpu.roll(phi, 127, 1)
            for (n, c), phi in list(state.items()):
                pull = pull_ref[2 * (i % 2) + n, c]
                side = side_ref[2 * (i % 2) + n, c]
                slope = None
                for low, high in (
                    (
                        phi_ref[2 * (i % 2) + n, c, PAD - 1 : PAD - 1 + ROWS, :],
                        phi_ref[2 * (i % 2) + n, c, PAD + 1 : PAD + 1 + ROWS, :],
                    ),
                    (
                        jnp.where(begins, after[n, (c - 1) % TILES], after[n, c]),
                        jnp.where(ends, ahead[n, (c + 1) % TILES], ahead[n, c]),
                    ),
                ):
                    steep = jnp.maximum(jnp.maximum(side * (phi - low), side * (phi - high)), 0.0)
                    slope = steep * steep if slope is None else slope + steep * steep
                grad = slope * lax.rsqrt(jnp.maximum(slope, 1e-30))
                state[n, c] = phi - pull * (grad - 1.0)
        for n, j in enumerate(fams):
            for c in range(TILES):
                phi_ref[2 * (i % 2) + n, c, PAD : PAD + ROWS, :] = state[n, c]
                done_ref[j, 0, :, c * 128 : (c + 1) * 128] = phi_ref[2 * (i % 2) + n, c, PAD + HALO : PAD + HALO + SLAB, :]
            pltpu.make_async_copy(done_ref.at[j], out_hbm.at[j], sems.at[j]).start()
        return carry

    for i in range(OWN // 2):
        pair(i, 0)
    for j in range(OWN):
        pltpu.make_async_copy(done_ref.at[j], out_hbm.at[j], sems.at[j]).wait()


VMEM = pl.BlockSpec(memory_space=pltpu.VMEM)
HBM = pl.BlockSpec(memory_space=pltpu.HBM)


def pinned(array):
    return pltpu.with_memory_space_constraint(array, pltpu.HBM)


def cost(flops):
    return pl.CostEstimate(flops=flops, bytes_accessed=10**6, transcendentals=0)


def call(kernel, name, ins, outs, scratch, room, estimate=None, where=None):
    return pl.pallas_call(
        kernel,
        out_shape=outs,
        in_specs=ins,
        out_specs=jax.tree.map(lambda _: VMEM, outs) if where is None else where,
        scratch_shapes=scratch,
        compiler_params=pltpu.CompilerParams(vmem_limit_bytes=room << 20),
        cost_estimate=estimate,
        name=name,
    )


def body(labels, family_of_grain):
    f32, bf16 = jnp.float32, jnp.bfloat16
    shape = jax.ShapeDtypeStruct
    lines = lax.axis_size(LINES)
    tables = smoothing_operator(NX)
    rows = jnp.asarray(mixing_rows(*tables, lax.axis_size(CHIPS)))
    high, low = (jnp.asarray(part) for part in tables)
    owner, left = call(
        lookup_kernel,
        "lookup",
        [HBM] * 3,
        (
            shape((lines, TILES // SIDES, SLAB, 128), bf16),
            shape((2 * WIDE, NX), jnp.float8_e4m3fn),
        ),
        [
            pltpu.VMEM((SLAB, NY), jnp.int32),
            pltpu.VMEM((GRAINS // 128, 128), jnp.int32),
            pltpu.SemaphoreType.DMA((3,)),
        ],
        4,
    )(
        pinned(labels.reshape(SLAB, NY)),
        pinned(family_of_grain.reshape(GRAINS // 128, 128)),
        pinned(rows),
    )
    owner = lax.all_to_all(owner, LINES, split_axis=0, concat_axis=0, tiled=True)
    sides = [owner, lax.ppermute(owner, "core", PARTNERS)]
    mixed = (shape((OTHERS * WIDE, NY // SIDES), bf16), shape((WIDE, NY // SIDES), f32))
    ids = [pltpu.VMEM((NX, NY // SIDES), jnp.int8)]
    (xa, na), (xb, nb) = (
        call(mix_kernel, "mix", [VMEM] * 2, mixed, ids, 8, cost(10**9))(side, left) for side in sides
    )
    keep, send = call(
        rank_kernel,
        "rank",
        [VMEM] * 5,
        (shape((2, ROWS, NY), f32), shape((2, ROWS, NY), f32)),
        [pltpu.VMEM((WIDE, NY), f32), pltpu.VMEM((2, WIDE, NY), f32)]
        + [pltpu.VMEM((max(CHUNKS) * WIDE, NY), f32)] * 2,
        16,
    )(xa, xb, na, nb, high)
    got = lax.ppermute(send, "core", PARTNERS)
    u = call(
        own_kernel,
        "own",
        [VMEM] * 4,
        shape((OWN * ROWS, NY), f32),
        [pltpu.VMEM((OWN * ROWS, NY), bf16), pltpu.VMEM((OWN * ROWS, NY), bf16)],
        8,
        cost(10**9),
    )(*sides, high, low)
    return call(
        sweep_kernel,
        "sweep",
        [VMEM] * 3,
        shape((OWN, 1, SLAB, NY), f32),
        [
            pltpu.VMEM((2, ROWS, NY), f32),
            pltpu.VMEM((4, TILES, PAD + ROWS + 8, 128), f32),
            pltpu.VMEM((4, TILES, ROWS, 128), f32),
            pltpu.VMEM((4, TILES, ROWS, 128), f32),
            pltpu.VMEM((OWN, 1, SLAB, NY), f32),
            pltpu.SemaphoreType.DMA((OWN,)),
        ],
        8,
        where=HBM,
    )(u, keep, got)


def solution(mesh):
    fine = Mesh(mesh.devices.reshape(2, 8, CORES, 8, 4), LINES + FAMS)
    return jax.shard_map(
        body,
        mesh=fine,
        in_specs=(P(None, LINES, None), P()),
        out_specs=P(FAMS, None, LINES, None),
        check_vma=False,
    )
```
